256 devices in a mesh: head: 8 (over y, core), tok: 32 (over x, z).
Axes of the slice: x: 4, y: 4, z: 8, core: 2. Of those that a mesh axis runs over, the one named last changes fastest.
Arguments:
- queries: bfloat16 [32768, 4096], P('tok', 'head'), may hold values from -100 to 100
- keys: bfloat16 [32768, 4096], P('tok', 'head'), may hold values from -6 to 6
- values: bfloat16 [32768, 4096], P('tok', 'head'), may hold values from -6 to 6
- step_size: float32 [32768, 8], P('tok', 'head'), may hold values from 6.1035156e-05 to 0.00061035156
- fast_one: bfloat16 [8, 512, 512], P('head'), may hold values from -0.25 to 0.25
- fast_three: bfloat16 [8, 512, 512], P('head'), may hold values from -0.25 to 0.25
- fast_two: bfloat16 [8, 512, 512], P('head'), may hold values from -0.25 to 0.25
- out_proj: bfloat16 [4096, 4096], P('tok', 'head'), may hold values from -0.09375 to 0.09375
- view_units: int32 [64], replicated, may hold values from 1 to 8, 256 in all
- evening: int32 [32, 32], P('tok'), may hold values from 0 to 31, each once within a row
Outputs:
- evened: bfloat16 [32768, 4096], P('tok', 'head')
The draws below stay inside these ranges and needn't reach their ends.
Inputs may be any that keep to these rules, and one draw needn't show every extreme that they name: `view_units`: the lengths sum to 256; the longest is exactly 8. `evening`: each row is a permutation of the token shards.
All inputs are finite; a program needn't handle non-finite values.
Results may differ from the reference program's by a relative error of at most 0.01.
The reference program's roundings to bfloat16 on the way count: a program that leaves them out, or rounds other values in their place, can miss the bound.
Values may be sent and summed in bfloat16 or wider, within the bound.
No kernel may reach another device: no remote copies, remote signals or barrier semaphores. Data moves between devices by JAX's collectives and lax.ppermute only.
A program may use at most 64 MiB of HBM per device.

```python
import math
import jax
import jax.numpy as jnp
import numpy as np
from jax import lax

D = 4096
HEADS = 8
DH = 512
FH = 512
TOK_DEV = 1024
VIEW_UNIT = 128
VIEW_MOST = 8
TOKENS = 32768
NVIEWS = 64
TILE = 32
N_TOK = 32


def draw_pair(key):
    base = jax.random.fold_in(key, 7)
    keys_raw = jnp.clip(jax.random.normal(jax.random.fold_in(base, 1), (TOKENS, D), jnp.float32), -6.0, 6.0)
    query_raw = jnp.clip(2.0 * jax.random.normal(jax.random.fold_in(base, 2), (TOKENS, D), jnp.float32), -12.0, 12.0)
    return (query_raw, keys_raw)


def draw_queries(key, part):
    return draw_pair(key)[0].astype(jnp.bfloat16)


def draw_keys(key, part):
    return draw_pair(key)[1].astype(jnp.bfloat16)


def block_levels(own_key, shape, split, smallest, high):
    factor_of, own = 1.0, jax.random.fold_in(own_key, 6)
    for axis_at, shards_of in split:
        steps = jnp.exp(jax.random.uniform(jax.random.fold_in(own, axis_at), (shards_of,), jnp.float32, smallest / len(split), high / len(split)))
        factor_of = factor_of * jnp.repeat(steps, shape[axis_at] // shards_of).reshape([-1 if axis == axis_at else 1 for axis in range(len(shape))])
    return factor_of


def profile(count, total, reach, skew):
    weights = [(1 << 20) // math.isqrt(grade ** skew) + 1 for grade in range(2, count + 1)]
    spare, given = total - reach - (count - 1), [1] * (count - 1)
    while spare > 0:
        candidates = [i for i in range(count - 1) if given[i] < reach]
        mass, budget = sum([weights[i] for i in candidates]), spare
        for i in candidates:
            addition = min(reach - given[i], max(1, budget * weights[i] // mass), spare)
            given[i] = given[i] + addition
            spare = spare - addition
    return np.array([reach] + given)


def ragged(stream_key, number_of, total, bound, lean):
    if number_of == 2:
        one = jax.random.randint(stream_key, (), max(1, total - bound), min(bound, total - 1) + 1)
        return jnp.stack([one, total - one])
    lengths = jnp.asarray(profile(number_of, total, bound, lean), jnp.int32)
    pairs = (number_of - 1) // 2
    giver, taker = lengths[1:1 + 2 * pairs:2], lengths[2:2 + 2 * pairs:2]
    margin = jnp.minimum(giver - 1, bound - taker)
    moved = jax.random.randint(jax.random.fold_in(stream_key, 1), (pairs,), 0, 1 << 20) % (margin + 1)
    lengths = lengths.at[1:1 + 2 * pairs:2].set(giver - moved).at[2:2 + 2 * pairs:2].set(taker + moved)
    return lengths[jax.random.permutation(jax.random.fold_in(stream_key, 2), number_of)]


def bell_draw(key, extent, deviation, bound, split=(), held_as=jnp.bfloat16):
    array = deviation * jax.random.normal(key, extent, jnp.float32)
    if split:
        array = array * block_levels(key, extent, split, -0.22, 0.18)
    return jnp.clip(array, -bound, bound).astype(held_as)


def setup_inputs(seed: int = 0) -> dict:
    seeds = jax.random.split(jax.random.key(seed), 11)
    return {
        "queries": draw_queries(jax.random.fold_in(seeds[10], 71), 0),
        "keys": draw_keys(jax.random.fold_in(seeds[10], 71), 0),
        "values": bell_draw(seeds[2], (TOKENS, D), 1.0, 6.0, ((0, 32), (1, 8))),
        "step_size": jnp.clip(jnp.exp(math.log(0.00061035156) - 2.3025851 * jax.random.uniform(seeds[3], (TOKENS, HEADS), jnp.float32) ** block_levels(seeds[3], (TOKENS, HEADS), ((0, 32), (1, 8)), -0.2, 0.2)), 6.103515625e-05, 0.00061035156),
        "fast_one": bell_draw(seeds[4], (HEADS, DH, FH), DH ** -0.5, 0.25, ((0, 8),)),
        "fast_three": bell_draw(seeds[5], (HEADS, DH, FH), DH ** -0.5, 0.25, ((0, 8),)),
        "fast_two": bell_draw(seeds[6], (HEADS, FH, DH), FH ** -0.5, 0.25, ((0, 8),)),
        "out_proj": bell_draw(seeds[7], (D, D), D ** -0.5, 0.09375, ((0, 32), (1, 8))),
        "view_units": ragged(seeds[8], NVIEWS, TOKENS // VIEW_UNIT, VIEW_MOST, 1).astype(jnp.int32),
        "evening": jax.vmap(lambda own: jax.random.permutation(own, N_TOK))(jax.random.split(seeds[9], N_TOK)).reshape((N_TOK, N_TOK)).astype(jnp.int32),
    }


def view_lookup(view_units, positions):
    view_ends = jnp.cumsum(view_units.astype(jnp.int32)).astype(jnp.int32) * VIEW_UNIT
    inside = (positions >= 0) & (positions < TOKENS)
    labels = lax.optimization_barrier(jnp.sum((positions[:, None] >= view_ends[None, :]).astype(jnp.int32), axis=1))
    return jnp.where(inside, labels, -1)

def rms_rows(rows):
    return rows * lax.rsqrt(lax.optimization_barrier(jnp.mean(rows * rows, axis=-1, keepdims=True)) + 1e-06)

def fast_head(operands):
    query_norm, key_norm, value_rows, rates, gate_w, up_w, down_w = operands
    gate_pre = jnp.dot(key_norm, gate_w, preferred_element_type=jnp.float32)
    up_pre = jnp.dot(key_norm, up_w, preferred_element_type=jnp.float32)
    gate_sig = jax.nn.sigmoid(gate_pre)
    hidden_keys = (gate_pre * gate_sig * up_pre).astype(jnp.bfloat16)
    descent = (-rates[:, None] * value_rows.astype(jnp.float32)).astype(jnp.bfloat16)
    grad_two = jnp.dot(hidden_keys.T, descent, preferred_element_type=jnp.float32)
    back = jnp.dot(descent, down_w.T, preferred_element_type=jnp.float32)
    grad_gate = (back * up_pre * gate_sig * (1.0 + gate_pre * (1.0 - gate_sig))).astype(jnp.bfloat16)
    grad_up = (back * gate_pre * gate_sig).astype(jnp.bfloat16)
    grad_one = jnp.dot(key_norm.T, grad_gate, preferred_element_type=jnp.float32)
    grad_three = jnp.dot(key_norm.T, grad_up, preferred_element_type=jnp.float32)
    new_one = (gate_w.astype(jnp.float32) - grad_one).astype(jnp.bfloat16)
    new_three = (up_w.astype(jnp.float32) - grad_three).astype(jnp.bfloat16)
    new_two = (down_w.astype(jnp.float32) - grad_two).astype(jnp.bfloat16)
    gate_q = jnp.dot(query_norm, new_one, preferred_element_type=jnp.float32)
    up_q = jnp.dot(query_norm, new_three, preferred_element_type=jnp.float32)
    hidden_q = (gate_q * jax.nn.sigmoid(gate_q) * up_q).astype(jnp.bfloat16)
    return jnp.dot(hidden_q, new_two, preferred_element_type=jnp.float32)

def reference(queries, keys, values, step_size, fast_one, fast_three, fast_two, out_proj, view_units, evening):
    scale = DH ** (-0.5)
    query_block = min(512, TOK_DEV)
    half_span = VIEW_MOST * VIEW_UNIT
    span = query_block + 2 * half_span
    key_pad = jnp.pad(keys, ((half_span, half_span), (0, 0)))
    value_pad = jnp.pad(values, ((half_span, half_span), (0, 0)))
    all_labels = view_lookup(view_units, jnp.arange(TOKENS + 2 * half_span, dtype=jnp.int32) - half_span)

    def attend(block_index):
        start = (block_index * query_block).astype(jnp.int32)
        query_rows = lax.dynamic_slice_in_dim(queries, start, query_block, 0).reshape(query_block, HEADS, DH)
        key_rows = lax.dynamic_slice_in_dim(key_pad, start, span, 0).reshape(span, HEADS, DH)
        value_rows = lax.dynamic_slice_in_dim(value_pad, start, span, 0).reshape(span, HEADS, DH)
        query_views = lax.dynamic_slice_in_dim(all_labels, start + half_span, query_block, 0)
        key_views = lax.dynamic_slice_in_dim(all_labels, start, span, 0)
        scores = jnp.einsum('qhd,khd->hqk', query_rows.astype(jnp.float32), key_rows.astype(jnp.float32)) * scale
        same_view = query_views[:, None] == key_views[None, :]
        scores = jnp.where(same_view[None], scores, -1e+30)
        top = lax.optimization_barrier(jnp.max(scores, axis=-1, keepdims=True))
        weights = jnp.exp(scores - top)
        probs = (weights / lax.optimization_barrier(jnp.sum(weights, axis=-1, keepdims=True))).astype(jnp.bfloat16)
        out_rows = jnp.einsum('hqk,khd->qhd', probs.astype(jnp.float32), value_rows.astype(jnp.float32))
        return out_rows.reshape(query_block, D)
    attended = lax.map(attend, jnp.arange(TOKENS // query_block, dtype=jnp.int32)).reshape(TOKENS, D)
    query_norm = rms_rows(queries.astype(jnp.float32).reshape(TOKENS, HEADS, DH)).astype(jnp.bfloat16)
    key_norm = rms_rows(keys.astype(jnp.float32).reshape(TOKENS, HEADS, DH)).astype(jnp.bfloat16)
    operands = (query_norm.transpose(1, 0, 2), key_norm.transpose(1, 0, 2), values.reshape(TOKENS, HEADS, DH).transpose(1, 0, 2), step_size.T, fast_one, fast_three, fast_two)
    fast_out = lax.map(fast_head, operands).transpose(1, 0, 2).reshape(TOKENS, D)
    mixed = (attended + fast_out).astype(jnp.bfloat16)
    projected = jnp.dot(mixed, out_proj, preferred_element_type=jnp.float32).astype(jnp.bfloat16)
    tiles = projected.reshape(N_TOK, N_TOK, TILE, D)
    match = (evening[:, :, None] == jnp.arange(N_TOK, dtype=jnp.int32)[None, None, :]).astype(jnp.int32)
    chosen = jnp.argmax(match, axis=1).astype(jnp.int32)
    picked = jnp.take_along_axis(tiles, chosen[:, :, None, None], axis=1)
    return picked.transpose(1, 0, 2, 3).reshape(TOKENS, D)
```

```python
import functools

import jax
import jax.numpy as jnp
from jax import lax
from jax.experimental import pallas as pl
from jax.experimental.pallas import tpu as pltpu
from jax.sharding import PartitionSpec as P

DH = 512
UNIT = 128
REACH = 7
TILE = 32
NX, NZ = 4, 8
NY, NC = 4, 2
CUT = DH // (NX * NZ)
BF = jnp.bfloat16
F32 = jnp.float32
VMEM_LIMIT = 60 * 1024 * 1024


def tok_shift(value, dx, dz):
    pairs = [
        (x * NZ + z, ((x + dx) % NX) * NZ + (z + dz) % NZ) for x in range(NX) for z in range(NZ)
    ]
    return lax.ppermute(value, "tok", pairs)


def shard_shift(value, step):
    count = NX * NZ
    return lax.ppermute(value, "tok", [(s, (s + step) % count) for s in range(count)])


def y_shift(value, dy):
    pairs = [(y * NC + c, ((y + dy) % NY) * NC + c) for y in range(NY) for c in range(NC)]
    return lax.ppermute(value, "head", pairs)


def core_swap(value):
    return lax.ppermute(value, "head", [(h, h ^ 1) for h in range(NY * NC)])


def x_shift(value, dx):
    return tok_shift(value, dx, 0)


def ring_of_four(block, shift):
    half = block.shape[0] // 2
    behind = shift(block, 1)
    ahead = shift(block, 3)
    first = shift(behind[:half], 1)
    second = shift(ahead[half:], 3)
    return behind, ahead, first, second


Z_GROUPS = [[x * NZ + z for z in range(NZ)] for x in range(NX)]


def z_exchange(value):
    return lax.all_to_all(
        value, "tok", split_axis=0, concat_axis=0, axis_index_groups=Z_GROUPS, tiled=True
    )


def rms(rows):
    rows = rows.astype(F32)
    return (rows * lax.rsqrt(jnp.mean(rows * rows, axis=-1, keepdims=True) + 1e-06)).astype(BF)


def mm(a, b):
    return jnp.dot(a, b, preferred_element_type=F32)


def mm_ta(a, b):
    return lax.dot_general(a, b, (((0,), (0,)), ((), ())), preferred_element_type=F32)


def mm_tb(a, b):
    return lax.dot_general(a, b, (((1,), (1,)), ((), ())), preferred_element_type=F32)


def grad_kernel(at, k, v, rate, one, three, two, own, s1a, s1b, s3a, s3b, r2a, r2b, acc):
    step = pl.program_id(0)

    @pl.when(step == 0)
    def _():
        acc[...] = jnp.zeros_like(acc)

    key_norm = rms(k[...])
    gate = mm(key_norm, one[0])
    up = mm(key_norm, three[0])
    sig = jax.nn.sigmoid(gate)
    silu = gate * sig
    hidden = (silu * up).astype(BF)
    descent = (-rate[...] * v[...].astype(F32)).astype(BF)
    back = mm_tb(descent, two[0])
    grad_gate = (back * up * sig * (1.0 + gate * (1.0 - sig))).astype(BF)
    grad_up = (back * silu).astype(BF)
    acc[0] += mm_ta(key_norm, grad_gate)
    acc[1] += mm_ta(key_norm, grad_up)
    acc[2] += mm_ta(hidden, descent)

    @pl.when(step == pl.num_programs(0) - 1)
    def _():
        def put(ref, quarter, lead, count):
            base = lax.rem(at[0] + quarter, NX) * (CUT * NZ) + lead * CUT
            for z in range(count):
                for m in range(3):
                    rows = acc[m, pl.ds(pl.multiple_of(base + z * CUT, CUT), CUT), :]
                    ref[(z * 3 + m) * CUT : (z * 3 + m + 1) * CUT, :] = rows.astype(ref.dtype)

        half = NZ // 2
        put(r2a, 2, 0, half)
        put(r2b, 2, half, half)
        put(s1a, 1, 0, half)
        put(s1b, 1, half, half)
        put(s3a, 3, 0, half)
        put(s3b, 3, half, half)
        put(own, 0, 0, NZ)


def gradients(x, keys, values, rate, one, three, two):
    rows = 256
    half = 3 * CUT * NZ // 2

    def piece(n, dtype):
        return jax.ShapeDtypeStruct((n, DH), dtype)

    shapes = [
        piece(2 * half, F32),
        piece(half, F32),
        piece(half, BF),
        piece(half, BF),
        piece(half, F32),
        piece(half, BF),
        piece(half, BF),
    ]
    whole = pl.BlockSpec((1, DH, DH), lambda i, *_: (0, 0, 0))
    return pl.pallas_call(
        grad_kernel,
        out_shape=shapes,
        grid_spec=pltpu.PrefetchScalarGridSpec(
            num_scalar_prefetch=1,
            grid=(keys.shape[0] // rows,),
            in_specs=[
                pl.BlockSpec((rows, DH), lambda i, *_: (i, 0)),
                pl.BlockSpec((rows, DH), lambda i, *_: (i, 0)),
                pl.BlockSpec((rows, 1), lambda i, *_: (i, 0)),
                whole,
                whole,
                whole,
            ],
            out_specs=[pl.BlockSpec(s.shape, lambda i, *_: (0, 0)) for s in shapes],
            scratch_shapes=[pltpu.VMEM((3, DH, DH), F32)],
        ),
        compiler_params=pltpu.CompilerParams(vmem_limit_bytes=VMEM_LIMIT),
        name="fast_gradients",
    )(x, keys, values, rate, one, three, two)


def attend_kernel(meta, q, k, v, left, right, out, k_win, v_win, sems):
    edge = REACH * UNIT
    rows = q.shape[0]
    copies = [
        pltpu.make_async_copy(left.at[pl.ds(0, edge)], k_win.at[pl.ds(0, edge)], sems.at[0]),
        pltpu.make_async_copy(k, k_win.at[pl.ds(edge, rows)], sems.at[1]),
        pltpu.make_async_copy(
            right.at[pl.ds(0, edge)], k_win.at[pl.ds(edge + rows, edge)], sems.at[2]
        ),
        pltpu.make_async_copy(left.at[pl.ds(edge, edge)], v_win.at[pl.ds(0, edge)], sems.at[3]),
        pltpu.make_async_copy(v, v_win.at[pl.ds(edge, rows)], sems.at[4]),
        pltpu.make_async_copy(
            right.at[pl.ds(edge, edge)], v_win.at[pl.ds(edge + rows, edge)], sems.at[5]
        ),
    ]
    for copy in copies:
        copy.start()
    for copy in copies:
        copy.wait()
    span = (REACH + 1) * UNIT
    units = rows // UNIT
    column = lax.broadcasted_iota(jnp.int32, (UNIT, span), 1)

    def unit(u, carry):
        first = pl.multiple_of(meta[u] * UNIT, UNIT)
        here = pl.ds(pl.multiple_of(u * UNIT, UNIT), UNIT)
        scores = mm_tb(q[here, :], k_win[pl.ds(first, span), :]) * (DH**-0.5)
        scores = jnp.where(column < meta[units + u] * UNIT, scores, -1e30)
        weights = jnp.exp(scores - jnp.max(scores, axis=-1, keepdims=True))
        total = jnp.sum(weights, axis=-1, keepdims=True)
        probs = (weights * (1.0 / total)).astype(BF)
        out[here, :] = mm(probs, v_win[pl.ds(first, span), :])
        return carry

    lax.fori_loop(0, units, unit, 0, unroll=2)


def attention(meta, queries, keys, values, left, right):
    rows = queries.shape[0]
    window = rows + 2 * REACH * UNIT
    anywhere = pl.BlockSpec(memory_space=pl.ANY)
    return pl.pallas_call(
        attend_kernel,
        out_shape=jax.ShapeDtypeStruct((rows, DH), F32),
        in_specs=[
            pl.BlockSpec(memory_space=pltpu.SMEM),
            pl.BlockSpec(memory_space=pltpu.VMEM),
            anywhere,
            anywhere,
            anywhere,
            anywhere,
        ],
        out_specs=pl.BlockSpec(memory_space=pltpu.VMEM),
        scratch_shapes=[
            pltpu.VMEM((window, DH), BF),
            pltpu.VMEM((window, DH), BF),
            pltpu.SemaphoreType.DMA((6,)),
        ],
        compiler_params=pltpu.CompilerParams(vmem_limit_bytes=VMEM_LIMIT),
        name="view_attention",
    )(meta, queries, keys, values, left, right)


def mix_kernel(at, place, q, attended, own, behind, ahead, first, second, out, fast):
    step = pl.program_id(0)

    @pl.when(step == 0)
    def _():
        def put(ref, quarter, lead):
            base = lax.rem(at[0] + quarter, NX) * (CUT * NZ) + lead * CUT
            for z in range(ref.shape[0] // (3 * CUT)):
                for m in range(3):
                    fast[m, pl.ds(pl.multiple_of(base + z * CUT, CUT), CUT), :] = ref[
                        (z * 3 + m) * CUT : (z * 3 + m + 1) * CUT, :
                    ]

        put(own, 0, 0)
        put(behind, 3, 0)
        put(ahead, 1, 0)
        put(first, 2, 0)
        put(second, 2, NZ // 2)

    query_norm = rms(q[...])
    gate = mm(query_norm, fast[0])
    up = mm(query_norm, fast[1])
    hidden = (gate * jax.nn.sigmoid(gate) * up).astype(BF)
    mixed = (attended[...] + mm(hidden, fast[2])).astype(BF)
    tiles = q.shape[0] // TILE
    for j in range(tiles):
        row = pl.multiple_of(place[step * tiles + j] * TILE, TILE)
        out[pl.ds(row, TILE), :] = mixed[j * TILE : (j + 1) * TILE, :]


def mix(x, place, queries, attended, pieces):
    rows = 256
    return pl.pallas_call(
        mix_kernel,
        out_shape=jax.ShapeDtypeStruct(queries.shape, BF),
        grid_spec=pltpu.PrefetchScalarGridSpec(
            num_scalar_prefetch=2,
            grid=(queries.shape[0] // rows,),
            in_specs=[
                pl.BlockSpec((rows, DH), lambda i, *_: (i, 0)),
                pl.BlockSpec((rows, DH), lambda i, *_: (i, 0)),
            ]
            + [pl.BlockSpec(p.shape, lambda i, *_: (0, 0)) for p in pieces],
            out_specs=pl.BlockSpec(queries.shape, lambda i, *_: (0, 0)),
            scratch_shapes=[pltpu.VMEM((3, DH, DH), BF)],
        ),
        compiler_params=pltpu.CompilerParams(vmem_limit_bytes=VMEM_LIMIT),
        name="fast_mix",
    )(x, place, queries, attended, *pieces)


def gather_projection(out_proj, x, z):
    rows = out_proj.shape[0]
    up = down = out_proj
    parts = {0: out_proj}
    for k in range(1, NZ // 2):
        up = tok_shift(up, 0, 1)
        down = tok_shift(down, 0, NZ - 1)
        parts[-k % NZ] = up
        parts[k] = down
    half = rows // 2
    parts[NZ // 2] = (tok_shift(up[:half], 0, 1), tok_shift(down[half:], 0, NZ - 1))
    pieces, where = [], []
    for k, part in parts.items():
        lead = lax.rem(z + k, NZ) * rows
        if isinstance(part, tuple):
            pieces += part
            where += [lead, lead + half]
        else:
            pieces.append(part)
            where.append(lead)
    column = place_rows(jnp.stack(where), pieces, rows * NZ)
    behind, ahead, first, second = ring_of_four(column, x_shift)
    tall = column.shape[0]
    opposite = lax.rem(x + 2, NX) * tall
    where = jnp.stack(
        [
            x * tall,
            lax.rem(x + 3, NX) * tall,
            lax.rem(x + 1, NX) * tall,
            opposite,
            opposite + tall // 2,
        ]
    )
    return place_rows(where, [column, behind, ahead, first, second], tall * NX)


def place_rows(where, pieces, total):
    count = len(pieces)

    def kernel(at, *refs):
        sources, out, sems = refs[:count], refs[count], refs[count + 1]
        copies = [
            pltpu.make_async_copy(
                source,
                out.at[pl.ds(pl.multiple_of(at[i], 16), source.shape[0])],
                sems.at[i],
            )
            for i, source in enumerate(sources)
        ]
        for copy in copies:
            copy.start()
        for copy in copies:
            copy.wait()

    anywhere = pl.BlockSpec(memory_space=pl.ANY)
    return pl.pallas_call(
        kernel,
        out_shape=jax.ShapeDtypeStruct((total, pieces[0].shape[1]), pieces[0].dtype),
        in_specs=[pl.BlockSpec(memory_space=pltpu.SMEM)] + [anywhere] * count,
        out_specs=anywhere,
        scratch_shapes=[pltpu.SemaphoreType.DMA((count,))],
        name="place_rows",
    )(where, *pieces)


def project_kernel(count, at, *refs):
    weights, blocks, out = refs[0], refs[1 : 1 + count], refs[1 + count]
    total = mm(blocks[0][...], weights[pl.ds(pl.multiple_of(at[0] * DH, DH), DH), :])
    for i in range(1, count):
        total += mm(blocks[i][...], weights[pl.ds(pl.multiple_of(at[i] * DH, DH), DH), :])
    out[...] = total


def project_near(heads, weights, blocks):
    rows = 256
    tokens = blocks[0].shape[0]
    return pl.pallas_call(
        functools.partial(project_kernel, len(blocks)),
        out_shape=jax.ShapeDtypeStruct((tokens, DH), F32),
        grid_spec=pltpu.PrefetchScalarGridSpec(
            num_scalar_prefetch=1,
            grid=(tokens // rows,),
            in_specs=[pl.BlockSpec(weights.shape, lambda i, *_: (0, 0))]
            + [pl.BlockSpec((rows, DH), lambda i, *_: (i, 0))] * len(blocks),
            out_specs=pl.BlockSpec((rows, DH), lambda i, *_: (i, 0)),
        ),
        compiler_params=pltpu.CompilerParams(vmem_limit_bytes=VMEM_LIMIT),
        name="project_near",
    )(heads, weights, *blocks)


def far_kernel(at, weights, near, f0, f1, s0, s1, out):
    step = pl.program_id(0)
    steps = pl.num_programs(0)

    def add(a, b):
        total = near[...] + mm(a[...], weights[pl.ds(pl.multiple_of(at[0] * DH, DH), DH), :])
        total += mm(b[...], weights[pl.ds(pl.multiple_of(at[1] * DH, DH), DH), :])
        out[...] = total.astype(out.dtype)

    @pl.when(step < steps // 2)
    def _():
        add(f0, f1)

    @pl.when(step >= steps // 2)
    def _():
        add(s0, s1)


def project_far(heads, weights, near, firsts, seconds):
    rows = 256
    steps = near.shape[0] // rows
    half = steps // 2
    lead = pl.BlockSpec((rows, DH), lambda i, *_: (jnp.minimum(i, half - 1), 0))
    tail = pl.BlockSpec((rows, DH), lambda i, *_: (jnp.maximum(i - half, 0), 0))
    block = pl.BlockSpec((rows, DH), lambda i, *_: (i, 0))
    return pl.pallas_call(
        far_kernel,
        out_shape=jax.ShapeDtypeStruct(near.shape, BF),
        grid_spec=pltpu.PrefetchScalarGridSpec(
            num_scalar_prefetch=1,
            grid=(steps,),
            in_specs=[
                pl.BlockSpec(weights.shape, lambda i, *_: (0, 0)),
                block,
                lead,
                lead,
                tail,
                tail,
            ],
            out_specs=block,
        ),
        compiler_params=pltpu.CompilerParams(vmem_limit_bytes=VMEM_LIMIT),
        name="project_far",
    )(heads, weights, near, *firsts, *seconds)


def view_spans(view_units, shard, units):
    count = view_units.shape[0]
    index = jnp.arange(count, dtype=jnp.int32)
    ends = jnp.sum(jnp.where(index[None, :] <= index[:, None], view_units[None, :], 0), axis=1)
    mine = shard * units + jnp.arange(units, dtype=jnp.int32)
    past = ends[None, :] <= mine[:, None]
    start = jnp.max(jnp.where(past, ends[None, :], 0), axis=1)
    stop = jnp.min(jnp.where(past, jnp.int32(1 << 30), ends[None, :]), axis=1)
    return jnp.concatenate([start - shard * units + REACH, stop - start])


def local(
    queries, keys, values, step_size, fast_one, fast_three, fast_two, out_proj, view_units, evening
):
    shard = lax.axis_index("tok").astype(jnp.int32)
    head = lax.axis_index("head").astype(jnp.int32)
    x, z = shard // NZ, lax.rem(shard, NZ)
    y, core = head // NC, lax.rem(head, NC)
    tokens = queries.shape[0]
    edge = REACH * UNIT

    left = shard_shift(jnp.concatenate([keys[tokens - edge :], values[tokens - edge :]]), 1)
    right = shard_shift(jnp.concatenate([keys[:edge], values[:edge]]), -1)

    x_at = x.reshape(1)
    own, s1a, s1b, s3a, s3b, r2a, r2b = gradients(
        x_at, keys, values, step_size, fast_one, fast_three, fast_two
    )
    from_behind = x_shift(r2a, 1).astype(F32)
    from_ahead = x_shift(r2b, 3).astype(F32)
    behind = x_shift(jnp.concatenate([(s1a + from_behind).astype(BF), s1b]), 1)
    ahead = x_shift(jnp.concatenate([s3a, (s3b + from_ahead).astype(BF)]), 3)
    quarter = (own + behind.astype(F32) + ahead.astype(F32)).astype(BF)
    parts = z_exchange(quarter).reshape(NZ, 3, CUT, DH)
    total = jnp.sum(parts.astype(F32), axis=0)
    old = jnp.stack(
        [
            lax.dynamic_slice(w, (0, shard * CUT, 0), (1, CUT, DH))[0]
            for w in (fast_one, fast_three, fast_two)
        ]
    )
    new = (old.astype(F32) - total).astype(BF).reshape(1, 3 * CUT, DH)
    block = z_exchange(jnp.broadcast_to(new, (NZ, 3 * CUT, DH)).reshape(NZ * 3 * CUT, DH))
    pieces = (block, *ring_of_four(block, x_shift))

    meta = view_spans(view_units, shard, tokens // UNIT)
    attended = attention(meta, queries, keys, values, left, right)
    mixed = mix(x_at, evening.reshape(-1), queries, attended, pieces)

    mine = lax.all_to_all(mixed, "tok", split_axis=0, concat_axis=0, tiled=True)

    weights = gather_projection(out_proj, x, z)

    behind, ahead, first, second = ring_of_four(mine, y_shift)
    near = [mine, behind, ahead]
    near_y = [y, lax.rem(y + 3, NY), lax.rem(y + 1, NY)]
    near += [core_swap(b) for b in near]
    heads = jnp.stack([v * NC + core for v in near_y] + [v * NC + 1 - core for v in near_y])
    partial = project_near(heads, weights, near)
    far_y = lax.rem(y + 2, NY) * NC
    far_heads = jnp.stack([far_y + core, far_y + 1 - core])
    return project_far(
        far_heads,
        weights,
        partial,
        (first, core_swap(first)),
        (second, core_swap(second)),
    )


def solution(mesh):
    return jax.shard_map(
        local,
        mesh=mesh,
        in_specs=(
            P("tok", "head"),
            P("tok", "head"),
            P("tok", "head"),
            P("tok", "head"),
            P("head", None, None),
            P("head", None, None),
            P("head", None, None),
            P("tok", "head"),
            P(),
            P("tok", None),
        ),
        out_specs=P("tok", "head"),
        check_vma=False,
    )
```

```python
import functools

import jax
import jax.numpy as jnp
from jax import lax
from jax.experimental import pallas as pl
from jax.experimental.pallas import tpu as pltpu
from jax.sharding import PartitionSpec as P


DH = 512
UNIT = 128
REACH = 7
TILE = 32
HALF_TILE = TILE // 2
NX, NZ = 4, 8
NY, NC = 4, 2
CUT = DH // (NX * NZ)
BF = jnp.bfloat16
F32 = jnp.float32
MIB = 1024 * 1024


def tok_shift(value, dx, dz):
    pairs = [
        (x * NZ + z, ((x + dx) % NX) * NZ + (z + dz) % NZ) for x in range(NX) for z in range(NZ)
    ]
    return lax.ppermute(value, "tok", pairs)


def shard_shift(value, step):
    count = NX * NZ
    return lax.ppermute(value, "tok", [(s, (s + step) % count) for s in range(count)])


def y_shift(value, dy):
    pairs = [(y * NC + c, ((y + dy) % NY) * NC + c) for y in range(NY) for c in range(NC)]
    return lax.ppermute(value, "head", pairs)


def core_swap(value):
    return lax.ppermute(value, "head", [(h, h ^ 1) for h in range(NY * NC)])


def x_shift(value, dx):
    return tok_shift(value, dx, 0)


def ring_of_four(block, shift):
    half = block.shape[0] // 2
    behind = shift(block, 1)
    ahead = shift(block, 3)
    first = shift(behind[:half], 1)
    second = shift(ahead[half:], 3)
    return behind, ahead, first, second


def ring_in_halves(blocks, shift):
    low, high = blocks
    behind = [shift(low, 1)]
    ahead = [shift(high, 3)]
    behind.append(shift(high, 1))
    ahead.insert(0, shift(low, 3))
    opposite = [shift(behind[0], 1), shift(ahead[1], 3)]
    return behind, ahead, opposite


Z_GROUPS = [[x * NZ + z for z in range(NZ)] for x in range(NX)]


def z_exchange(value):
    return lax.all_to_all(
        value, "tok", split_axis=0, concat_axis=0, axis_index_groups=Z_GROUPS, tiled=True
    )


def rms(rows):
    rows = rows.astype(F32)
    return (rows * lax.rsqrt(jnp.mean(rows * rows, axis=-1, keepdims=True) + 1e-06)).astype(BF)


def mm(a, b):
    return jnp.dot(a, b, preferred_element_type=F32)


def mm_ta(a, b):
    return lax.dot_general(a, b, (((0,), (0,)), ((), ())), preferred_element_type=F32)


def mm_tb(a, b):
    return lax.dot_general(a, b, (((1,), (1,)), ((), ())), preferred_element_type=F32)


def grad_kernel(at, k, v, rate, one, three, two, own, mid_a, mid_b, send_a, send_b, acc):
    step = pl.program_id(0)

    @pl.when(step == 0)
    def _():
        acc[...] = jnp.zeros_like(acc)

    key_norm = rms(k[...])
    gate = mm(key_norm, one[0])
    up = mm(key_norm, three[0])
    sig = jax.nn.sigmoid(gate)
    silu = gate * sig
    hidden = (silu * up).astype(BF)
    lanes = rate.shape[1]
    rates = []
    for i in range(k.shape[0] // lanes):
        row = rate[pl.ds(step * (k.shape[0] // lanes) + i, 1), :]
        column = jnp.transpose(jnp.broadcast_to(row, (lanes, lanes)))
        rates.append(jnp.concatenate([column] * (DH // lanes), axis=1))
    descent = (-jnp.concatenate(rates, axis=0) * v[...].astype(F32)).astype(BF)
    back = mm_tb(descent, two[0])
    grad_gate = (back * up * sig * (1.0 + gate * (1.0 - sig))).astype(BF)
    grad_up = (back * silu).astype(BF)
    acc[0] += mm_ta(key_norm, grad_gate)
    acc[1] += mm_ta(key_norm, grad_up)
    acc[2] += mm_ta(hidden, descent)

    @pl.when(step == pl.num_programs(0) - 1)
    def _():
        half = NZ // 2

        def put(ref, quarter, lead, count, to=0):
            base = lax.rem(at[0] + quarter, NX) * (CUT * NZ) + lead * CUT
            for z in range(count):
                for m in range(3):
                    rows = acc[m, pl.ds(pl.multiple_of(base + z * CUT, CUT), CUT), :]
                    here = ((to + z) * 3 + m) * CUT
                    ref[here : here + CUT, :] = rows.astype(ref.dtype)

        put(send_a, 2, 0, half)
        put(send_a, 1, half, half, half)
        put(send_b, 2, half, half)
        put(send_b, 3, 0, half, half)
        put(mid_a, 1, 0, half)
        put(mid_b, 3, half, half)
        put(own, 0, 0, NZ)


def gradients(x, keys, values, rate, one, three, two):
    rows = 256
    half = 3 * CUT * NZ // 2

    def piece(n, dtype):
        return jax.ShapeDtypeStruct((n, DH), dtype)

    shapes = [
        piece(2 * half, F32),
        piece(half, F32),
        piece(half, F32),
        piece(2 * half, BF),
        piece(2 * half, BF),
    ]
    whole = pl.BlockSpec((1, DH, DH), lambda i, *_: (0, 0, 0))
    return pl.pallas_call(
        grad_kernel,
        out_shape=shapes,
        grid_spec=pltpu.PrefetchScalarGridSpec(
            num_scalar_prefetch=1,
            grid=(keys.shape[0] // rows,),
            in_specs=[
                pl.BlockSpec((rows, DH), lambda i, *_: (i, 0)),
                pl.BlockSpec((rows, DH), lambda i, *_: (i, 0)),
                pl.BlockSpec(rate.shape, lambda i, *_: (0, 0)),
                whole,
                whole,
                whole,
            ],
            out_specs=[pl.BlockSpec(s.shape, lambda i, *_: (0, 0)) for s in shapes],
            scratch_shapes=[pltpu.VMEM((3, DH, DH), F32)],
        ),
        compiler_params=pltpu.CompilerParams(vmem_limit_bytes=18 * MIB),
        name="fast_gradients",
    )(x, *[pltpu.with_memory_space_constraint(v, pltpu.HBM) for v in (keys, values, rate, one, three, two)])


def in_vmem(kernel, shapes, *args, mib=8, scalars=0):
    vmem, smem = (pl.BlockSpec(memory_space=m) for m in (pltpu.VMEM, pltpu.SMEM))
    return pl.pallas_call(
        kernel,
        out_shape=shapes,
        in_specs=[smem] * scalars + [vmem] * (len(args) - scalars),
        out_specs=jax.tree.map(lambda _: pl.BlockSpec(memory_space=pltpu.VMEM), shapes),
        compiler_params=pltpu.CompilerParams(vmem_limit_bytes=mib * MIB),
    )(*args)


def relay_kernel(mid_a, mid_b, got_a, got_b, out_a, out_b):
    half = mid_a.shape[0]
    out_a[...] = (mid_a[...] + got_a[:half, :].astype(F32)).astype(BF)
    out_b[...] = (mid_b[...] + got_b[:half, :].astype(F32)).astype(BF)


def quarter_kernel(own, got_a, got_b, last_a, last_b, out):
    half = last_a.shape[0]
    low = own[:half, :] + last_a[...].astype(F32) + got_b[half:, :].astype(F32)
    high = own[half:, :] + got_a[half:, :].astype(F32) + last_b[...].astype(F32)
    out[:half, :] = low.astype(BF)
    out[half:, :] = high.astype(BF)


def update_kernel(at, parts, one, three, two, out):
    rows = 3 * CUT
    total = parts[0:rows, :].astype(F32)
    for i in range(1, NZ):
        total += parts[i * rows : (i + 1) * rows, :].astype(F32)
    for m, old in enumerate((one, three, two)):
        new = (old[0].astype(F32) - total[m * CUT : (m + 1) * CUT, :]).astype(BF)
        for i in range(NZ):
            out[i * rows + m * CUT : i * rows + (m + 1) * CUT, :] = new


def update(shard, parts, one, three, two):
    slab = pl.BlockSpec((1, CUT, DH), lambda i, at: (0, at[0], 0))
    whole = pl.BlockSpec(parts.shape, lambda i, at: (0, 0))
    return pl.pallas_call(
        update_kernel,
        out_shape=jax.ShapeDtypeStruct(parts.shape, BF),
        grid_spec=pltpu.PrefetchScalarGridSpec(
            num_scalar_prefetch=1,
            grid=(1,),
            in_specs=[whole, slab, slab, slab],
            out_specs=whole,
        ),
        compiler_params=pltpu.CompilerParams(vmem_limit_bytes=4 * MIB),
        name="fast_update",
    )(shard, parts, one, three, two)


def attend_kernel(meta, q, k, v, k_left, k_right, v_left, v_right, out, k_win, v_win, sems):
    edge = REACH * UNIT
    rows = q.shape[0]
    copies = []
    for i, (win, left, mine, right) in enumerate(
        ((k_win, k_left, k, k_right), (v_win, v_left, v, v_right))
    ):
        copies += [
            pltpu.make_async_copy(
                left.at[pl.ds(rows - edge, edge)], win.at[pl.ds(0, edge)], sems.at[3 * i]
            ),
            pltpu.make_async_copy(mine, win.at[pl.ds(edge, rows)], sems.at[3 * i + 1]),
            pltpu.make_async_copy(
                right.at[pl.ds(0, edge)], win.at[pl.ds(edge + rows, edge)], sems.at[3 * i + 2]
            ),
        ]
    for copy in copies:
        copy.start()
    for copy in copies:
        copy.wait()
    span = (REACH + 1) * UNIT
    units = rows // UNIT
    column = lax.broadcasted_iota(jnp.int32, (UNIT, span), 1)

    def unit(u, carry):
        first = pl.multiple_of(meta[u] * UNIT, UNIT)
        here = pl.ds(pl.multiple_of(u * UNIT, UNIT), UNIT)
        scores = mm_tb(q[here, :], k_win[pl.ds(first, span), :]) * (DH**-0.5)
        scores = jnp.where(column < meta[units + u] * UNIT, scores, -1e30)
        weights = jnp.exp(scores - jnp.max(scores, axis=-1, keepdims=True))
        total = jnp.sum(weights, axis=-1, keepdims=True)
        probs = (weights * (1.0 / total)).astype(BF)
        out[here, :] = mm(probs, v_win[pl.ds(first, span), :])
        return carry

    lax.fori_loop(0, units, unit, 0)


def attention(meta, queries, keys, values, *edges):
    rows = queries.shape[0]
    window = rows + 2 * REACH * UNIT
    anywhere = pl.BlockSpec(memory_space=pl.ANY)
    return pl.pallas_call(
        attend_kernel,
        out_shape=jax.ShapeDtypeStruct((rows, DH), F32),
        in_specs=[
            pl.BlockSpec(memory_space=pltpu.SMEM),
            pl.BlockSpec(memory_space=pltpu.VMEM),
        ]
        + [anywhere] * 6,
        out_specs=pl.BlockSpec(memory_space=pltpu.VMEM),
        scratch_shapes=[
            pltpu.VMEM((window, DH), BF),
            pltpu.VMEM((window, DH), BF),
            pltpu.SemaphoreType.DMA((6,)),
        ],
        compiler_params=pltpu.CompilerParams(vmem_limit_bytes=18 * MIB),
        name="view_attention",
    )(meta, queries, keys, values, *edges)


def mix_kernel(at, place, q, attended, own, behind, ahead, first, second, a0, a1, b0, b1, fast):
    step = pl.program_id(0)

    @pl.when(step == 0)
    def _():
        def put(ref, quarter, lead):
            base = lax.rem(at[0] + quarter, NX) * (CUT * NZ) + lead * CUT
            for z in range(ref.shape[0] // (3 * CUT)):
                for m in range(3):
                    fast[m, pl.ds(pl.multiple_of(base + z * CUT, CUT), CUT), :] = ref[
                        (z * 3 + m) * CUT : (z * 3 + m + 1) * CUT, :
                    ]

        put(own, 0, 0)
        put(behind, 3, 0)
        put(ahead, 1, 0)
        put(first, 2, 0)
        put(second, 2, NZ // 2)

    query_norm = rms(q[...])
    gate = mm(query_norm, fast[0])
    up = mm(query_norm, fast[1])
    hidden = (gate * jax.nn.sigmoid(gate) * up).astype(BF)
    mixed = (attended[...] + mm(hidden, fast[2])).astype(BF)
    tiles = q.shape[0] // TILE
    for j in range(tiles):
        to = place[step * tiles + j]
        cut = j * TILE + HALF_TILE
        for half, (a, b) in enumerate(((a0, b0), (a1, b1))):

            @pl.when(to // (NX * NZ // 2) == half)
            def _(to=to - half * (NX * NZ // 2), a=a, b=b, cut=cut):
                row = pl.multiple_of(to * HALF_TILE, HALF_TILE)
                a[pl.ds(row, HALF_TILE), :] = mixed[cut - HALF_TILE : cut, :]
                b[pl.ds(row, HALF_TILE), :] = mixed[cut : cut + HALF_TILE, :]


def mix(x, place, queries, attended, pieces):
    rows = 128
    return pl.pallas_call(
        mix_kernel,
        out_shape=[jax.ShapeDtypeStruct((queries.shape[0] // 4, DH), BF)] * 4,
        grid_spec=pltpu.PrefetchScalarGridSpec(
            num_scalar_prefetch=2,
            grid=(queries.shape[0] // rows,),
            in_specs=[
                pl.BlockSpec((rows, DH), lambda i, *_: (i, 0)),
                pl.BlockSpec((rows, DH), lambda i, *_: (i, 0)),
            ]
            + [pl.BlockSpec(p.shape, lambda i, *_: (0, 0)) for p in pieces],
            out_specs=[pl.BlockSpec((queries.shape[0] // 4, DH), lambda i, *_: (0, 0))] * 4,
            scratch_shapes=[pltpu.VMEM((3, DH, DH), BF)],
        ),
        compiler_params=pltpu.CompilerParams(vmem_limit_bytes=14 * MIB),
        name="fast_mix",
    )(x, place, queries, attended, *pieces)


def gather_projection(out_proj, x, z):
    rows = out_proj.shape[0]
    up = down = out_proj
    parts = {0: out_proj}
    for k in range(1, NZ // 2):
        up = tok_shift(up, 0, 1)
        down = tok_shift(down, 0, NZ - 1)
        parts[-k % NZ] = up
        parts[k] = down
    half = rows // 2
    parts[NZ // 2] = (tok_shift(up[:half], 0, 1), tok_shift(down[half:], 0, NZ - 1))
    pieces, where = [], []
    for k, part in parts.items():
        lead = lax.rem(z + k, NZ) * rows
        if isinstance(part, tuple):
            pieces += part
            where += [lead, lead + half]
        else:
            pieces.append(part)
            where.append(lead)
    column = place_rows(jnp.stack(where), pieces, rows * NZ, 2)
    behind, ahead, opposite = ring_in_halves(column, x_shift)
    half = rows * NZ // 2
    pieces, where = [], []
    for blocks, away in ((column, 0), (behind, 3), (ahead, 1), (opposite, 2)):
        pieces += blocks
        lead = lax.rem(x + away, NX) * (2 * half)
        where += [lead, lead + half]
    return place_rows(jnp.stack(where), pieces, 2 * half * NX)[0]


def place_rows(where, pieces, total, cuts=1):
    count = len(pieces)
    rows = total // cuts

    def kernel(at, *refs):
        for i, source in enumerate(refs[:count]):
            tall = source.shape[0]
            for cut, out in enumerate(refs[count:]):

                @pl.when(at[i] // rows == cut)
                def _(out=out, cut=cut, source=source, i=i, tall=tall):
                    out[pl.ds(pl.multiple_of(at[i] - cut * rows, 16), tall), :] = source[...]

    shape = jax.ShapeDtypeStruct((rows, pieces[0].shape[1]), pieces[0].dtype)
    return in_vmem(kernel, [shape] * cuts, where, *pieces, mib=12, scalars=1)


def by_chunks(rows, body):
    chunk = 128

    def step(i, carry):
        body(pl.multiple_of(i * chunk, chunk), chunk)
        return carry

    lax.fori_loop(0, rows // chunk, step, 0)


def near_kernel(count, at, weights, *refs):
    blocks, out = refs[:-1], refs[-1]
    rows = blocks[0].shape[0]
    for group in range(len(blocks) // count):

        def body(start, size, group=group):
            total = None
            for i in range(count):
                head = weights[pl.ds(pl.multiple_of(at[i] * DH, DH), DH), :]
                product = mm(blocks[group * count + i][pl.ds(start, size), :], head)
                total = product if total is None else total + product
            out[pl.ds(group * rows + start, size), :] = total

        by_chunks(rows, body)


def far_kernel(at, weights, near, *refs):
    blocks, out = refs[:-1], refs[-1]
    rows = blocks[0].shape[0]
    for group in range(len(blocks) // 2):

        def body(start, size, group=group):
            here = pl.ds(group * rows + start, size)
            total = near[here, :]
            for i in range(2):
                head = weights[pl.ds(pl.multiple_of(at[i] * DH, DH), DH), :]
                total += mm(blocks[group * 2 + i][pl.ds(start, size), :], head)
            out[here, :] = total.astype(out.dtype)

        by_chunks(rows, body)


def view_spans(view_units, shard, units):
    count = view_units.shape[0]
    index = jnp.arange(count, dtype=jnp.int32)
    ends = jnp.sum(jnp.where(index[None, :] <= index[:, None], view_units[None, :], 0), axis=1)
    mine = shard * units + jnp.arange(units, dtype=jnp.int32)
    past = ends[None, :] <= mine[:, None]
    start = jnp.max(jnp.where(past, ends[None, :], 0), axis=1)
    stop = jnp.min(jnp.where(past, jnp.int32(1 << 30), ends[None, :]), axis=1)
    return jnp.concatenate([start - shard * units + REACH, stop - start])


def local(
    queries, keys, values, step_size, fast_one, fast_three, fast_two, out_proj, view_units, evening
):
    shard = lax.axis_index("tok").astype(jnp.int32)
    head = lax.axis_index("head").astype(jnp.int32)
    x, z = shard // NZ, lax.rem(shard, NZ)
    y, core = head // NC, lax.rem(head, NC)
    tokens = queries.shape[0]

    k_left, k_right = shard_shift(keys, 1), shard_shift(keys, -1)
    v_left, v_right = shard_shift(values, 1), shard_shift(values, -1)

    x_at = x.reshape(1)
    own, mid_a, mid_b, send_a, send_b = gradients(
        x_at, keys, values, step_size.reshape(-1, 128), fast_one, fast_three, fast_two
    )
    got_a, got_b = x_shift(send_a, 1), x_shift(send_b, 3)
    last_a, last_b = in_vmem(
        relay_kernel, [jax.ShapeDtypeStruct(mid_a.shape, BF)] * 2, mid_a, mid_b, got_a, got_b
    )
    last_a, last_b = x_shift(last_a, 1), x_shift(last_b, 3)
    quarter = in_vmem(
        quarter_kernel, jax.ShapeDtypeStruct(own.shape, BF), own, got_a, got_b, last_a, last_b
    )
    parts = z_exchange(quarter)
    copies = update(shard.reshape(1), parts, fast_one, fast_three, fast_two)
    block = z_exchange(copies)
    pieces = (block, *ring_of_four(block, x_shift))

    weights = gather_projection(out_proj, x, z)

    meta = view_spans(view_units, shard, tokens // UNIT)
    attended = attention(
        meta, queries, keys, values, k_left, k_right, v_left, v_right
    )
    a0, a1, b0, b1 = mix(x_at, evening.reshape(-1), queries, attended, pieces)

    far_y = lax.rem(y + 2, NY) * NC
    near_y = [y, lax.rem(y + 3, NY), lax.rem(y + 1, NY)]
    near_heads = jnp.stack(
        [v * NC + core for v in near_y] + [v * NC + 1 - core for v in near_y]
    )
    far_heads = jnp.stack([far_y + core, far_y + 1 - core])

    def project(mine):
        behind, ahead, opposite = ring_in_halves(mine, y_shift)
        near, far = [], []
        for i in range(2):
            own = [mine[i], behind[i], ahead[i]]
            near += own + [core_swap(b) for b in own]
            far += [opposite[i], core_swap(opposite[i])]
        rows = 2 * mine[0].shape[0]
        partial = in_vmem(
            functools.partial(near_kernel, 6),
            jax.ShapeDtypeStruct((rows, DH), F32),
            near_heads,
            weights,
            *near,
            mib=12,
            scalars=1,
        )
        return in_vmem(
            far_kernel,
            jax.ShapeDtypeStruct((rows, DH), BF),
            far_heads,
            weights,
            partial,
            *far,
            mib=10,
            scalars=1,
        )

    def exchange(value):
        return lax.all_to_all(value, "tok", split_axis=0, concat_axis=0, tiled=True)

    half_b = exchange(jnp.concatenate([b0, b1]))
    half_a = project((a0, a1))
    half_a = exchange(half_a)
    middle = half_b.shape[0] // 2
    half_b = project((half_b[:middle], half_b[middle:]))
    count = tokens // TILE
    both = [h.reshape(count, 1, HALF_TILE, DH) for h in (half_a, half_b)]
    return jnp.concatenate(both, axis=1).reshape(tokens, DH)


def solution(mesh):
    return jax.shard_map(
        local,
        mesh=mesh,
        in_specs=(
            P("tok", "head"),
            P("tok", "head"),
            P("tok", "head"),
            P("tok", "head"),
            P("head", None, None),
            P("head", None, None),
            P("head", None, None),
            P("tok", "head"),
            P(),
            P("tok", None),
        ),
        out_specs=P("tok", "head"),
        check_vma=False,
    )
```
